32 devices in a mesh: groups: 2 (over y), rows: 16 (over z, x, core).
Axes of the slice: x: 2, y: 2, z: 4, core: 2. Of those that a mesh axis runs over, the one named last changes fastest.
Arguments:
- factor_panel: bfloat16 [32768, 2048], P(('groups', 'rows')), parts along dimension 0, may hold values from -0.0625 to 0.0625
- later_adjoint: bfloat16 [32768, 1024], P(('groups', 'rows')), parts along dimension 0, may hold values from -6 to 6
- saved_solution: bfloat16 [32768, 1024], P(('groups', 'rows')), parts along dimension 0, may hold values from -6 to 6
- cotangent: float32 [4096, 1024], P(('groups', 'rows')), parts along dimension 0, may hold values from -6 to 6
- inverse_block: bfloat16 [4096, 2048], P(('groups', 'rows')), parts along dimension 0, as said below
Outputs:
- panel_adjoint: bfloat16 [4096, 1024], P(('groups', 'rows')), parts along dimension 0
- factor_grad: bfloat16 [32768, 2048], P(('groups', 'rows')), parts along dimension 0
The draws below stay inside these ranges and needn't reach their ends.
There are 2 independent parts, one for each index of `groups`. The reference program is written for one: setup_inputs(seed, part) draws one part's arguments, and reference() takes and returns one part's arrays. A program takes and returns all parts, laid end to end along the dimension named above; each array names one. Nothing has to cross between parts.
Inputs may be any that keep to these rules, and one draw needn't show every extreme that they name: inverse_block is zero below its diagonal.
All inputs are finite; a program needn't handle non-finite values.
Results may differ from the reference program's by a relative error of at most 0.0057.
Values may be sent and summed in bfloat16 or wider, within the bound.
No kernel may reach another device: no remote copies, remote signals or barrier semaphores. Data moves between devices by JAX's collectives and lax.ppermute only.
A program may use at most 64 MiB of HBM per device.

```python
import jax
import jax.numpy as jnp
from jax import lax

PANEL = 2048
SIDES = 1024
ORDER = 16384


def draw_inverse_block(key, part):
    first, second = jax.random.split(jax.random.fold_in(key, 7), 2)
    row_index = jnp.arange(PANEL)[:, None]
    col_index = jnp.arange(PANEL)[None, :]
    diag_vals = jnp.exp(jax.random.uniform(first, (PANEL, 1), jnp.float32, -0.69, 0.69))
    off_vals = jax.random.normal(second, (PANEL, PANEL), jnp.float32) * 0.6 * (1.0 / PANEL) ** 0.5
    upper = jnp.where(col_index > row_index, off_vals, 0.0)
    diagonal = jnp.where(col_index == row_index, diag_vals, 0.0)
    return (upper + diagonal).astype(jnp.bfloat16)


def spiked(values, rng, source, target, blocks, factor):
    owner, partner = [(jnp.arange(values.shape[axis_at]) // (values.shape[axis_at] // blocks)).reshape([-1 if axis == axis_at else 1 for axis in range(values.ndim)]) for axis_at in (source, target)]
    chosen = jax.random.permutation(rng, blocks)[partner]
    strong = (owner == chosen) | (owner == (partner + blocks // 2) % blocks)
    return jnp.where(strong, factor * values, values)


def steps_of(key, dims, cuts, smallest, top_value):
    level = 1.0
    for position, blocks in cuts:
        heights = jax.random.uniform(jax.random.fold_in(jax.random.fold_in(key, 6), position), (blocks,), jnp.float32, smallest / len(cuts), top_value / len(cuts))
        level = level * jnp.repeat(jnp.exp(heights), dims[position] // blocks).reshape((-1,) + (1,) * (len(dims) - 1 - position))
    return level


def normal_values(own_key, shape, width, bound, cuts=(), dtype=jnp.bfloat16):
    array = jax.random.normal(own_key, shape, jnp.float32) * width
    if len(cuts) > 0:
        array = steps_of(own_key, shape, cuts, -0.22, 0.18) * array
    return jnp.clip(array, min=-bound, max=bound).astype(dtype)


def bell_draw_with(rng, shape, width, most, pieces, heavy, kind=jnp.bfloat16):
    result = width * jax.random.normal(rng, shape, jnp.float32)
    if pieces:
        result = result * steps_of(rng, shape, pieces, -0.22, 0.18)
    return jnp.clip(spiked(result, jax.random.fold_in(rng, 3), *heavy), -most, most).astype(kind)


def setup_inputs(seed: int = 0, part: int = 0) -> dict:
    streams_of = jax.random.split(jax.random.key(seed), 6)
    own_keys = jax.random.split(jax.random.fold_in(streams_of[5], part), 6)
    return {
        "factor_panel": bell_draw_with(own_keys[0], (ORDER, PANEL), ORDER ** -0.5, 0.0625, ((0, 16),), (0, 1, 16, 2.0)),
        "later_adjoint": normal_values(own_keys[1], (ORDER, SIDES), 1.0, 6.0, ((0, 16),)),
        "saved_solution": normal_values(own_keys[2], (ORDER, SIDES), 1.0, 6.0, ((0, 16),)),
        "cotangent": normal_values(own_keys[3], (PANEL, SIDES), 1.0, 6.0, ((0, 16),), jnp.float32),
        "inverse_block": draw_inverse_block(jax.random.fold_in(jax.random.fold_in(streams_of[5], part), 71), part),
    }


def reference(factor_panel, later_adjoint, saved_solution, cotangent, inverse_block):
    products = lax.dot_general(factor_panel, later_adjoint, (((0,), (0,)), ((), ())), preferred_element_type=jnp.float32)
    residual = (cotangent - products).astype(jnp.bfloat16)
    panel_adjoint = jnp.dot(inverse_block, residual, preferred_element_type=jnp.float32).astype(jnp.bfloat16)
    outer = lax.dot_general(saved_solution, panel_adjoint, (((1,), (1,)), ((), ())), preferred_element_type=jnp.float32)
    factor_grad = (-outer).astype(jnp.bfloat16)
    return panel_adjoint, factor_grad
```

```python
import functools

import jax
import jax.numpy as jnp
from jax import lax
from jax.experimental import pallas as pl
from jax.experimental.pallas import tpu as pltpu
from jax.sharding import PartitionSpec as P


BF, F32 = jnp.bfloat16, jnp.float32
SIZES = (64, 64)
STARTS = tuple(sum(SIZES[:k]) for k in range(len(SIZES)))
CHUNKS = len(SIZES)
VMEM = 24 << 20
FIRST_VMEM = 20 << 20
OUTER_VMEM = 16 << 20


def dot(a, b, ca, cb):
    return lax.dot_general(a, b, (((ca,), (cb,)), ((), ())), preferred_element_type=F32)


def cost(flops, moved):
    return pl.CostEstimate(flops=flops, bytes_accessed=moved, transcendentals=0)


def call(kernel, out_shape, grid, in_specs, out_specs, scratch, flops, moved, limit=VMEM):
    return pl.pallas_call(
        kernel,
        out_shape=out_shape,
        grid_spec=pltpu.PrefetchScalarGridSpec(
            num_scalar_prefetch=1,
            grid=grid,
            in_specs=in_specs,
            out_specs=out_specs,
            scratch_shapes=scratch,
        ),
        compiler_params=pltpu.CompilerParams(vmem_limit_bytes=limit),
        cost_estimate=cost(flops, moved),
    )


WHOLE = pl.BlockSpec(memory_space=pltpu.VMEM)
SCALARS = pl.BlockSpec(memory_space=pltpu.SMEM)


def once(kernel, out_shape, n_in, scratch, flops, moved, limit=VMEM, aliases={}):
    many = isinstance(out_shape, tuple)
    return pl.pallas_call(
        kernel,
        out_shape=out_shape,
        in_specs=[SCALARS] + [WHOLE] * n_in,
        out_specs=(WHOLE,) * len(out_shape) if many else WHOLE,
        scratch_shapes=scratch,
        input_output_aliases=aliases,
        compiler_params=pltpu.CompilerParams(vmem_limit_bytes=limit),
        cost_estimate=cost(flops, moved),
    )


TILE = 512


def first_kernel(groups, ids, l, f, c, *refs):
    n = 2 * len(groups)
    outs, (lv, fv, cv, lt, sems) = refs[:n * CHUNKS], refs[n * CHUNKS:]
    w = l.shape[1] // 8
    own = c.shape[0]
    tiles = f.shape[1] // TILE
    lefts, cots, rights = [], [], []
    for j in range(n):
        at = pl.ds(pl.multiple_of((ids[0] ^ (groups[j // 2] + j % 2)) * w, 128), w)
        lefts.append(pltpu.make_async_copy(l.at[:, at], lv.at[j], sems.at[j]))
        cots.append(pltpu.make_async_copy(c.at[:, at], cv.at[j], sems.at[n + j]))
    for t in range(tiles):
        rights.append(pltpu.make_async_copy(f.at[:, t * TILE:(t + 1) * TILE], fv.at[t], sems.at[2 * n + t]))
    for copy in lefts + rights + cots:
        copy.start()
    for j in range(n):
        lefts[j].wait()
        lt[j * w:(j + 1) * w, :] = lv[j].T
    for t in range(tiles):
        rights[t].wait()
        acc = -dot(lt[...], fv[t], 1, 0)
        if t == 0:
            for copy in cots:
                copy.wait()
        for j in range(n):
            for k in range(CHUNKS):
                out = outs[(j // 2 * CHUNKS + k) * 2 + j % 2]
                at = j * w + STARTS[k]
                out[:, t * TILE:(t + 1) * TILE] = acc[at:at + SIZES[k]].astype(out.dtype)
        for u in range(TILE // own):
            @pl.when(ids[2] == t * (TILE // own) + u)
            def _():
                for j in range(n):
                    both = acc[j * w:(j + 1) * w, u * own:(u + 1) * own] + cv[j].T
                    for k in range(CHUNKS):
                        out = outs[(j // 2 * CHUNKS + k) * 2 + j % 2]
                        got = both[STARTS[k]:STARTS[k] + SIZES[k]]
                        out[:, t * TILE + u * own:t * TILE + (u + 1) * own] = got.astype(out.dtype)


def first(ids, later, panel, cot, groups):
    rows, width = panel.shape
    sides = later.shape[1]
    w = sides // 8
    own = cot.shape[0]
    n = 2 * len(groups)
    shapes = ()
    for _ in groups:
        for s in SIZES:
            shapes += (jax.ShapeDtypeStruct((s, width), F32), jax.ShapeDtypeStruct((s, width), BF))
    return pl.pallas_call(
        functools.partial(first_kernel, groups),
        out_shape=shapes,
        in_specs=[SCALARS] + [pl.BlockSpec(memory_space=pltpu.HBM)] * 3,
        out_specs=(WHOLE,) * len(shapes),
        scratch_shapes=[
            pltpu.VMEM((n, rows, w), BF),
            pltpu.VMEM((width // TILE, rows, TILE), BF),
            pltpu.VMEM((n, own, w), F32),
            pltpu.VMEM((n * w, rows), BF),
            pltpu.SemaphoreType.DMA((2 * n + width // TILE,)),
        ],
        compiler_params=pltpu.CompilerParams(vmem_limit_bytes=FIRST_VMEM),
        cost_estimate=cost(2 * n * w * rows * width, 4 * rows * width),
        name="first",
    )(ids, *(pltpu.with_memory_space_constraint(a, pltpu.HBM) for a in (later, panel, cot)))


def again_kernel(groups, ids, l, f, c, *refs):
    n = len(groups)
    outs, lt = refs[:2 * n * CHUNKS], refs[2 * n * CHUNKS]
    w = l.shape[1] // 8
    own = c.shape[0]
    width = f.shape[1]
    for j in range(2 * n):
        q = groups[j // 2] + j % 2
        at = pl.ds(pl.multiple_of((ids[0] ^ q) * w, 128), w)
        lt[j * w:(j + 1) * w, :] = l[:, at].T
    tile = 512
    for t in range(0, width, tile):
        acc = -dot(lt[...], f[:, t:t + tile], 1, 0)
        for g in range(n):
            for k in range(CHUNKS):
                for s in range(2):
                    out = outs[(g * CHUNKS + k) * 2 + s]
                    at = (2 * g + s) * w + STARTS[k]
                    out[:, t:t + tile] = acc[at:at + SIZES[k]].astype(out.dtype)
        for u in range(tile // own):
            @pl.when(ids[2] == t // own + u)
            def _():
                for j in range(2 * n):
                    q = groups[j // 2] + j % 2
                    rows = c[:, pl.ds(pl.multiple_of((ids[0] ^ q) * w, 128), w)].T
                    both = acc[j * w:(j + 1) * w, u * own:(u + 1) * own] + rows
                    for k in range(CHUNKS):
                        out = outs[(j // 2 * CHUNKS + k) * 2 + j % 2]
                        got = both[STARTS[k]:STARTS[k] + SIZES[k]]
                        out[:, t + u * own:t + (u + 1) * own] = got.astype(out.dtype)


def again(ids, later, panel, cot, groups):
    rows, width = panel.shape
    sides = later.shape[1]
    n = len(groups)
    shapes = ()
    for _ in groups:
        for s in SIZES:
            shapes += (jax.ShapeDtypeStruct((s, width), F32), jax.ShapeDtypeStruct((s, width), BF))
    return once(
        functools.partial(again_kernel, groups),
        shapes,
        3,
        [pltpu.VMEM((n * sides // 4, rows), BF)],
        rows * sides * width * n // 2,
        5 * rows * width,
        FIRST_VMEM,
    )(ids, later, panel, cot)


def order_kernel(ids, s, out):
    w = s.shape[1] // 8
    at = 0
    for k, q in ORDER:
        block = s[:, pl.ds(pl.multiple_of((ids[0] ^ q) * w, 128), w)]
        out[:, at:at + SIZES[k]] = block[:, STARTS[k]:STARTS[k] + SIZES[k]]
        at += SIZES[k]


def order(ids, saved):
    rows, sides = saved.shape
    tile = 256
    return call(
        order_kernel,
        jax.ShapeDtypeStruct((rows, sides), BF),
        (rows // tile,),
        [pl.BlockSpec((tile, sides), lambda t, i: (t, 0))],
        pl.BlockSpec((tile, sides), lambda t, i: (t, 0)),
        [],
        0,
        4 * rows * sides,
    )(ids, saved)


def gather_kernel(places, ids, *refs):
    out = refs[-1]
    for (q, at, size), ref in zip(places, refs):
        own = 128
        out[pl.ds(pl.multiple_of((ids[0] ^ q) * own + at, 16), size), :] = ref[...]


def gather(ids, parts):
    places = tuple((q, at, a.shape[0]) for q, at, a in parts)
    width = parts[0][2].shape[1]
    return call(
        functools.partial(gather_kernel, places),
        jax.ShapeDtypeStruct((8 * 128, width), BF),
        (1,),
        [pl.BlockSpec(a.shape, lambda t, i: (0, 0)) for _, _, a in parts],
        pl.BlockSpec((8 * 128, width), lambda t, i: (0, 0)),
        [],
        0,
        32 * 128 * width,
    )(ids, *[a for _, _, a in parts])


def middle_kernel(ids, r, inv, out):
    out[...] = dot(r[...], inv[...], 1, 1).astype(BF)


def middle(ids, r, inv):
    m, width = r.shape
    n = inv.shape[0]
    return call(
        middle_kernel,
        jax.ShapeDtypeStruct((m, n), BF),
        (1,),
        [pl.BlockSpec((m, width), lambda t, i: (0, 0)), pl.BlockSpec((n, width), lambda t, i: (0, 0))],
        pl.BlockSpec((m, n), lambda t, i: (0, 0)),
        [],
        2 * m * width * n,
        2 * n * width,
    )(ids, r, inv)


def outer_kernel(n_in, lo, first, ids, s, *refs):
    pieces, refs = refs[:n_in], refs[n_in:]
    out = refs[-1]
    depth = sum(p.shape[0] for p in pieces)
    half = out.shape[1] // 2
    for h in range(2):
        for t in range(0, half, 512):
            rhs = jnp.concatenate([p[:, h * half + t:h * half + t + 512] for p in pieces], axis=0)
            got = dot(s[:, lo:lo + depth], rhs, 1, 0)
            at = pl.ds(pl.multiple_of((ids[1] ^ h) * half + t, 512), 512)
            if first:
                out[:, at] = got
            else:
                out[:, at] = refs[0][:, at] + got


def outer(ids, saved, pieces, lo, acc=None):
    rows = saved.shape[0]
    width = pieces[0].shape[1]
    part = sum(p.shape[0] for p in pieces)
    return once(
        functools.partial(outer_kernel, len(pieces), lo, acc is None),
        jax.ShapeDtypeStruct((rows, width), F32),
        1 + len(pieces) + (acc is not None),
        [],
        2 * rows * part * width,
        4 * rows * width,
        OUTER_VMEM,
        {} if acc is None else {2 + len(pieces): 0},
    )(ids, saved, *pieces, *(() if acc is None else (acc,)))


def last_kernel(n_in, lo, ids, s, acc, *refs):
    blocks, (out, adj, held, sems) = refs[:-4], refs[-4:]
    pieces = [blocks[k * 8 + q] for k, q in ORDER[-n_in:]]
    depth = sum(p.shape[0] for p in pieces)
    half = acc.shape[1] // 2
    tiles, tile = held.shape[0], held.shape[2]
    w = adj.shape[1] // 8
    own = adj.shape[0]
    copies = []
    for t in range(tiles):
        h, inner = divmod(t * tile, half)
        at = pl.ds(pl.multiple_of((ids[1] ^ h) * half + inner, tile), tile)
        rhs = jnp.concatenate([p[:, t * tile:(t + 1) * tile] for p in pieces], axis=0)
        held[t] = (-(acc[:, at] + dot(s[:, lo:lo + depth], rhs, 1, 0))).astype(BF)
        copies.append(pltpu.make_async_copy(held.at[t], out.at[:, at], sems.at[t]))
        copies[-1].start()
    mine = pl.ds(pl.multiple_of(ids[0] * own, 128), own)
    for q in range(8):
        block = jnp.concatenate([blocks[k * 8 + q][:, mine] for k in range(CHUNKS)], axis=0)
        adj[:, pl.ds(pl.multiple_of((ids[0] ^ q) * w, 128), w)] = block.T
    for copy in copies:
        copy.wait()


def last(ids, saved, acc, pieces, n_in, lo, own):
    rows, width = acc.shape
    sides = sum(SIZES) * 8
    tiles = 4
    return pl.pallas_call(
        functools.partial(last_kernel, n_in, lo),
        out_shape=(jax.ShapeDtypeStruct((rows, width), BF), jax.ShapeDtypeStruct((own, sides), BF)),
        in_specs=[SCALARS] + [WHOLE] * (2 + len(pieces)),
        out_specs=(pl.BlockSpec(memory_space=pltpu.HBM), WHOLE),
        scratch_shapes=[pltpu.VMEM((tiles, rows, width // tiles), BF), pltpu.SemaphoreType.DMA((tiles,))],
        compiler_params=pltpu.CompilerParams(vmem_limit_bytes=OUTER_VMEM),
        cost_estimate=cost(2 * rows * n_in * pieces[-1].shape[0] * width, 4 * rows * width),
        name="last",
    )(ids, saved, acc, *pieces)


ORDER = (
    (0, 0), (0, 1), (1, 0), (1, 1), (0, 2), (0, 3), (0, 4), (0, 5),
    (1, 2), (1, 3), (1, 4), (1, 5), (0, 6), (0, 7), (1, 6), (1, 7),
)
TAKES = (4, 4, 4, 4)


def make_tiled(n):
    def swap(a, bit):
        return lax.ppermute(a, "rows", [(i, i ^ bit) for i in range(n)])

    def body(factor_panel, later_adjoint, saved_solution, cotangent, inverse_block):
        me = lax.axis_index("rows").astype(jnp.int32)
        own = cotangent.shape[0]
        ids = jnp.stack([me % 8, me // 8, me])

        half = own // 2
        again_inverse = lax.optimization_barrier(inverse_block)
        i2a = swap(inverse_block[:half], 2)
        i4 = swap(inverse_block, 4)
        i2b = swap(again_inverse[half:], 2)
        i6z = swap(i2a, 4)
        i6x = swap(i4[half:], 2)
        firsts = first(ids, later_adjoint, factor_panel, cotangent, (6, 4))
        firsts += again(ids, later_adjoint, factor_panel, cotangent, (2, 0))
        shards = []
        for q, at, a in ((0, 0, inverse_block), (4, 0, i4), (2, 0, i2a), (2, half, i2b), (6, 0, i6z), (6, half, i6x)):
            shards += [(q, at, a), (q + 1, at, swap(a, 1))]
        saved = order(ids, saved_solution)
        inv = gather(ids, shards)

        pieces = []
        acc = None
        for k in range(CHUNKS):
            kept = {}
            for j, g in enumerate((6, 4, 2, 0)):
                keep, send = firsts[(j * CHUNKS + k) * 2:(j * CHUNKS + k) * 2 + 2]
                kept[g] = keep + swap(send, 1).astype(F32)
            u4 = kept[4] + swap(kept[6].astype(BF), 2).astype(F32)
            u0 = kept[0] + swap(kept[2].astype(BF), 2).astype(F32)
            r = u0 + swap(u4.astype(BF), 4).astype(F32)
            r = (r + swap(r.astype(BF), 8).astype(F32)).astype(BF)
            pt = middle(ids, r, inv)
            p = {0: jnp.concatenate([pt, swap(pt, 8)], axis=1)}
            p[2] = swap(p[0], 2)
            p[4] = swap(p[0], 4)
            p[6] = swap(p[4], 2) if k < CHUNKS - 1 else swap(p[2], 4)
            for g in (0, 2, 4, 6):
                p[g + 1] = swap(p[g], 1)
            pieces.append([p[q] for q in range(8)])
        at = lo = 0
        for take in TAKES[:-1]:
            using = [pieces[c][q] for c, q in ORDER[at:at + take]]
            acc = outer(ids, saved, using, lo, acc)
            at += take
            lo += sum(p.shape[0] for p in using)
        grad, adj = last(ids, saved, acc, sum(pieces, []), TAKES[-1], lo, own)
        return adj, grad

    return body


def make_body(n):
    def swap(a, bit):
        return lax.ppermute(a, "rows", [(i, i ^ bit) for i in range(n)])

    rest = [8 << k for k in range(16) if 8 << k < n]

    def body(factor_panel, later_adjoint, saved_solution, cotangent, inverse_block):
        me = lax.axis_index("rows")
        low = me % 8
        sides, panel, own = later_adjoint.shape[1], factor_panel.shape[1], cotangent.shape[0]
        w = sides // 8

        def cols(a, q):
            return lax.dynamic_slice(a, (0, (low ^ q) * w), (a.shape[0], w))

        inv4 = swap(inverse_block, 4)
        kept = {}
        for g in (6, 2, 4, 0):
            pair = jnp.concatenate([cols(later_adjoint, g), cols(later_adjoint, g ^ 1)], axis=1)
            prod = dot(pair, factor_panel, 0, 0)
            cot = jnp.concatenate([cols(cotangent, g), cols(cotangent, g ^ 1)], axis=1).T
            base = lax.dynamic_update_slice(jnp.zeros((2 * w, panel), F32), cot, (0, me * own))
            both = base - prod
            got = swap(both[w:].astype(BF), 1)
            kept[g] = both[:w] + got.astype(F32)
        u4 = kept[4] + swap(kept[6].astype(BF), 2).astype(F32)
        u0 = kept[0] + swap(kept[2].astype(BF), 2).astype(F32)
        r = u0 + swap(u4.astype(BF), 4).astype(F32)
        shards = {0: inverse_block, 4: inv4, 2: swap(inverse_block, 2), 6: swap(inv4, 2)}
        inv = jnp.zeros((8 * own, panel), BF)
        for q in (0, 4, 2, 6):
            inv = lax.dynamic_update_slice(inv, shards[q], ((low ^ q) * own, 0))
            inv = lax.dynamic_update_slice(inv, swap(shards[q], 1), ((low ^ q ^ 1) * own, 0))
        for b in rest:
            r = r + swap(r.astype(BF), b).astype(F32)
        pt = dot(r.astype(BF), inv, 1, 1).astype(BF)
        for b in rest:
            other = swap(pt, b)
            up = (me // b) % 2
            pt = jnp.where(up == 1, jnp.concatenate([other, pt], 1), jnp.concatenate([pt, other], 1))
        p = {0: pt}
        p[2] = swap(pt, 2)
        p[4] = swap(pt, 4)
        p[6] = swap(p[4], 2)
        for g in (0, 4, 2, 6):
            p[g ^ 1] = swap(p[g], 1)
        left = jnp.concatenate([cols(saved_solution, q) for q in range(8)], axis=1)
        grad = -dot(left, jnp.concatenate([p[q] for q in range(8)], axis=0), 1, 0)
        adj = jnp.zeros((own, sides), BF)
        for q in range(8):
            mine = lax.dynamic_slice(p[q], (0, me * own), (w, own)).T
            adj = lax.dynamic_update_slice(adj, mine, (0, (low ^ q) * w))
        return adj, grad.astype(BF)

    return body


def solution(mesh):
    n = mesh.shape["rows"]
    placed = P(("groups", "rows"), None)
    return jax.shard_map(
        make_tiled(n) if n == 16 else make_body(n),
        mesh=mesh,
        in_specs=(placed,) * 5,
        out_specs=(placed, placed),
        check_vma=False,
    )
```

```python
import functools

import jax
import jax.numpy as jnp
from jax import lax
from jax.experimental import pallas as pl
from jax.experimental.pallas import tpu as pltpu
from jax.sharding import PartitionSpec as P


BF, F32 = jnp.bfloat16, jnp.float32
SIZES = (64, 64)
STARTS = tuple(sum(SIZES[:k]) for k in range(len(SIZES)))
CHUNKS = len(SIZES)
VMEM = 24 << 20
FIRST_VMEM = 20 << 20
OUTER_VMEM = 16 << 20


def dot(a, b, ca, cb):
    return lax.dot_general(a, b, (((ca,), (cb,)), ((), ())), preferred_element_type=F32)


def cost(flops, moved):
    return pl.CostEstimate(flops=flops, bytes_accessed=moved, transcendentals=0)


def call(kernel, out_shape, grid, in_specs, out_specs, scratch, flops, moved, limit=VMEM):
    return pl.pallas_call(
        kernel,
        out_shape=out_shape,
        grid_spec=pltpu.PrefetchScalarGridSpec(
            num_scalar_prefetch=1,
            grid=grid,
            in_specs=in_specs,
            out_specs=out_specs,
            scratch_shapes=scratch,
        ),
        compiler_params=pltpu.CompilerParams(vmem_limit_bytes=limit),
        cost_estimate=cost(flops, moved),
    )


WHOLE = pl.BlockSpec(memory_space=pltpu.VMEM)
SCALARS = pl.BlockSpec(memory_space=pltpu.SMEM)


def once(kernel, out_shape, n_in, scratch, flops, moved, limit=VMEM, aliases={}):
    many = isinstance(out_shape, tuple)
    return pl.pallas_call(
        kernel,
        out_shape=out_shape,
        in_specs=[SCALARS] + [WHOLE] * n_in,
        out_specs=(WHOLE,) * len(out_shape) if many else WHOLE,
        scratch_shapes=scratch,
        input_output_aliases=aliases,
        compiler_params=pltpu.CompilerParams(vmem_limit_bytes=limit),
        cost_estimate=cost(flops, moved),
    )


TILE = 512


def first_kernel(groups, ids, l, f, c, *refs):
    n = 2 * len(groups)
    outs, (lv, fv, cv, lt, sems) = refs[:n * CHUNKS], refs[n * CHUNKS:]
    w = l.shape[1] // 8
    own = c.shape[0]
    tiles = f.shape[1] // TILE
    lefts, cots, rights = [], [], []
    for j in range(n):
        at = pl.ds(pl.multiple_of((ids[0] ^ (groups[j // 2] + j % 2)) * w, 128), w)
        lefts.append(pltpu.make_async_copy(l.at[:, at], lv.at[j], sems.at[j]))
        cots.append(pltpu.make_async_copy(c.at[:, at], cv.at[j], sems.at[n + j]))
    for t in range(tiles):
        rights.append(pltpu.make_async_copy(f.at[:, t * TILE:(t + 1) * TILE], fv.at[t], sems.at[2 * n + t]))
    for copy in lefts + rights + cots:
        copy.start()
    for j in range(n):
        lefts[j].wait()
        lt[j * w:(j + 1) * w, :] = lv[j].T
    for t in range(tiles):
        rights[t].wait()
        acc = -dot(lt[...], fv[t], 1, 0)
        if t == 0:
            for copy in cots:
                copy.wait()
        for j in range(n):
            for k in range(CHUNKS):
                out = outs[(j // 2 * CHUNKS + k) * 2 + j % 2]
                at = j * w + STARTS[k]
                out[:, t * TILE:(t + 1) * TILE] = acc[at:at + SIZES[k]].astype(out.dtype)
        for u in range(TILE // own):
            @pl.when(ids[2] == t * (TILE // own) + u)
            def _():
                for j in range(n):
                    both = acc[j * w:(j + 1) * w, u * own:(u + 1) * own] + cv[j].T
                    for k in range(CHUNKS):
                        out = outs[(j // 2 * CHUNKS + k) * 2 + j % 2]
                        got = both[STARTS[k]:STARTS[k] + SIZES[k]]
                        out[:, t * TILE + u * own:t * TILE + (u + 1) * own] = got.astype(out.dtype)


def first(ids, later, panel, cot, groups):
    rows, width = panel.shape
    sides = later.shape[1]
    w = sides // 8
    own = cot.shape[0]
    n = 2 * len(groups)
    shapes = ()
    for _ in groups:
        for s in SIZES:
            shapes += (jax.ShapeDtypeStruct((s, width), F32), jax.ShapeDtypeStruct((s, width), BF))
    return pl.pallas_call(
        functools.partial(first_kernel, groups),
        out_shape=shapes,
        in_specs=[SCALARS] + [pl.BlockSpec(memory_space=pltpu.HBM)] * 3,
        out_specs=(WHOLE,) * len(shapes),
        scratch_shapes=[
            pltpu.VMEM((n, rows, w), BF),
            pltpu.VMEM((width // TILE, rows, TILE), BF),
            pltpu.VMEM((n, own, w), F32),
            pltpu.VMEM((n * w, rows), BF),
            pltpu.SemaphoreType.DMA((2 * n + width // TILE,)),
        ],
        compiler_params=pltpu.CompilerParams(vmem_limit_bytes=FIRST_VMEM),
        cost_estimate=cost(2 * n * w * rows * width, 4 * rows * width),
        name="first",
    )(ids, *(pltpu.with_memory_space_constraint(a, pltpu.HBM) for a in (later, panel, cot)))


def again_kernel(groups, ids, l, f, c, *refs):
    n = len(groups)
    outs, lt = refs[:2 * n * CHUNKS], refs[2 * n * CHUNKS]
    w = l.shape[1] // 8
    own = c.shape[0]
    width = f.shape[1]
    for j in range(2 * n):
        q = groups[j // 2] + j % 2
        at = pl.ds(pl.multiple_of((ids[0] ^ q) * w, 128), w)
        lt[j * w:(j + 1) * w, :] = l[:, at].T
    tile = 512
    for t in range(0, width, tile):
        acc = -dot(lt[...], f[:, t:t + tile], 1, 0)
        for g in range(n):
            for k in range(CHUNKS):
                for s in range(2):
                    out = outs[(g * CHUNKS + k) * 2 + s]
                    at = (2 * g + s) * w + STARTS[k]
                    out[:, t:t + tile] = acc[at:at + SIZES[k]].astype(out.dtype)
        for u in range(tile // own):
            @pl.when(ids[2] == t // own + u)
            def _():
                for j in range(2 * n):
                    q = groups[j // 2] + j % 2
                    rows = c[:, pl.ds(pl.multiple_of((ids[0] ^ q) * w, 128), w)].T
                    both = acc[j * w:(j + 1) * w, u * own:(u + 1) * own] + rows
                    for k in range(CHUNKS):
                        out = outs[(j // 2 * CHUNKS + k) * 2 + j % 2]
                        got = both[STARTS[k]:STARTS[k] + SIZES[k]]
                        out[:, t + u * own:t + (u + 1) * own] = got.astype(out.dtype)


def again(ids, later, panel, cot, groups):
    rows, width = panel.shape
    sides = later.shape[1]
    n = len(groups)
    shapes = ()
    for _ in groups:
        for s in SIZES:
            shapes += (jax.ShapeDtypeStruct((s, width), F32), jax.ShapeDtypeStruct((s, width), BF))
    return once(
        functools.partial(again_kernel, groups),
        shapes,
        3,
        [pltpu.VMEM((n * sides // 4, rows), BF)],
        rows * sides * width * n // 2,
        5 * rows * width,
        FIRST_VMEM,
    )(ids, later, panel, cot)


def order_kernel(ids, s, out):
    w = s.shape[1] // 8
    at = 0
    for k, q in ORDER:
        block = s[:, pl.ds(pl.multiple_of((ids[0] ^ q) * w, 128), w)]
        out[:, at:at + SIZES[k]] = block[:, STARTS[k]:STARTS[k] + SIZES[k]]
        at += SIZES[k]


def order(ids, saved):
    rows, sides = saved.shape
    tile = 256
    return call(
        order_kernel,
        jax.ShapeDtypeStruct((rows, sides), BF),
        (rows // tile,),
        [pl.BlockSpec((tile, sides), lambda t, i: (t, 0))],
        pl.BlockSpec((tile, sides), lambda t, i: (t, 0)),
        [],
        0,
        4 * rows * sides,
    )(ids, saved)


def gather_kernel(places, ids, *refs):
    out = refs[-1]
    for (q, at, size), ref in zip(places, refs):
        own = 128
        out[pl.ds(pl.multiple_of((ids[0] ^ q) * own + at, 16), size), :] = ref[...]


def gather(ids, parts):
    places = tuple((q, at, a.shape[0]) for q, at, a in parts)
    width = parts[0][2].shape[1]
    return call(
        functools.partial(gather_kernel, places),
        jax.ShapeDtypeStruct((8 * 128, width), BF),
        (1,),
        [pl.BlockSpec(a.shape, lambda t, i: (0, 0)) for _, _, a in parts],
        pl.BlockSpec((8 * 128, width), lambda t, i: (0, 0)),
        [],
        0,
        32 * 128 * width,
    )(ids, *[a for _, _, a in parts])


def middle_kernel(ids, r, inv, out):
    out[...] = dot(r[...], inv[...], 1, 1).astype(BF)


def middle(ids, r, inv):
    m, width = r.shape
    n = inv.shape[0]
    return call(
        middle_kernel,
        jax.ShapeDtypeStruct((m, n), BF),
        (1,),
        [pl.BlockSpec((m, width), lambda t, i: (0, 0)), pl.BlockSpec((n, width), lambda t, i: (0, 0))],
        pl.BlockSpec((m, n), lambda t, i: (0, 0)),
        [],
        2 * m * width * n,
        2 * n * width,
    )(ids, r, inv)


def outer_kernel(n_in, lo, first, ids, s, *refs):
    pieces, refs = refs[:n_in], refs[n_in:]
    out = refs[-1]
    depth = sum(p.shape[0] for p in pieces)
    half = out.shape[1] // 2
    for h in range(2):
        for t in range(0, half, 512):
            rhs = jnp.concatenate([p[:, h * half + t:h * half + t + 512] for p in pieces], axis=0)
            got = dot(s[:, lo:lo + depth], rhs, 1, 0)
            at = pl.ds(pl.multiple_of((ids[1] ^ h) * half + t, 512), 512)
            if first:
                out[:, at] = got
            else:
                out[:, at] = refs[0][:, at] + got


def outer(ids, saved, pieces, lo, acc=None):
    rows = saved.shape[0]
    width = pieces[0].shape[1]
    part = sum(p.shape[0] for p in pieces)
    return once(
        functools.partial(outer_kernel, len(pieces), lo, acc is None),
        jax.ShapeDtypeStruct((rows, width), F32),
        1 + len(pieces) + (acc is not None),
        [],
        2 * rows * part * width,
        4 * rows * width,
        OUTER_VMEM,
        {} if acc is None else {2 + len(pieces): 0},
    )(ids, saved, *pieces, *(() if acc is None else (acc,)))


def last_kernel(n_in, lo, ids, s, acc, *refs):
    blocks, (out, adj, held, sems) = refs[:-4], refs[-4:]
    pieces = [blocks[k * 8 + q] for k, q in ORDER[-n_in:]]
    depth = sum(p.shape[0] for p in pieces)
    half = acc.shape[1] // 2
    tiles, tile = held.shape[0], held.shape[2]
    w = adj.shape[1] // 8
    own = adj.shape[0]
    copies = []
    for t in range(tiles):
        h, inner = divmod(t * tile, half)
        at = pl.ds(pl.multiple_of((ids[1] ^ h) * half + inner, tile), tile)
        rhs = jnp.concatenate([p[:, t * tile:(t + 1) * tile] for p in pieces], axis=0)
        held[t] = (-(acc[:, at] + dot(s[:, lo:lo + depth], rhs, 1, 0))).astype(BF)
        copies.append(pltpu.make_async_copy(held.at[t], out.at[:, at], sems.at[t]))
        copies[-1].start()
    mine = pl.ds(pl.multiple_of(ids[0] * own, 128), own)
    for q in range(8):
        block = jnp.concatenate([blocks[k * 8 + q][:, mine] for k in range(CHUNKS)], axis=0)
        adj[:, pl.ds(pl.multiple_of((ids[0] ^ q) * w, 128), w)] = block.T
    for copy in copies:
        copy.wait()


def last(ids, saved, acc, pieces, n_in, lo, own):
    rows, width = acc.shape
    sides = sum(SIZES) * 8
    tiles = 4
    return pl.pallas_call(
        functools.partial(last_kernel, n_in, lo),
        out_shape=(jax.ShapeDtypeStruct((rows, width), BF), jax.ShapeDtypeStruct((own, sides), BF)),
        in_specs=[SCALARS] + [WHOLE] * (2 + len(pieces)),
        out_specs=(pl.BlockSpec(memory_space=pltpu.HBM), WHOLE),
        scratch_shapes=[pltpu.VMEM((tiles, rows, width // tiles), BF), pltpu.SemaphoreType.DMA((tiles,))],
        compiler_params=pltpu.CompilerParams(vmem_limit_bytes=OUTER_VMEM),
        cost_estimate=cost(2 * rows * n_in * pieces[-1].shape[0] * width, 4 * rows * width),
        name="last",
    )(ids, saved, acc, *pieces)


def upper_kernel(inv, out, sem):
    copy = pltpu.make_async_copy(inv.at[:out.shape[0]], out, sem)
    copy.start()
    copy.wait()


def upper(inverse):
    rows, width = inverse.shape
    return pl.pallas_call(
        upper_kernel,
        out_shape=jax.ShapeDtypeStruct((rows // 2, width), BF),
        in_specs=[pl.BlockSpec(memory_space=pltpu.HBM)],
        out_specs=WHOLE,
        scratch_shapes=[pltpu.SemaphoreType.DMA(())],
        compiler_params=pltpu.CompilerParams(vmem_limit_bytes=2 << 20),
        cost_estimate=cost(0, rows * width),
        name="upper",
    )(pltpu.with_memory_space_constraint(inverse, pltpu.HBM))


ORDER = (
    (0, 0), (0, 1), (1, 0), (1, 1), (0, 2), (0, 3), (0, 4), (0, 5),
    (1, 2), (1, 3), (1, 4), (1, 5), (0, 6), (0, 7), (1, 6), (1, 7),
)
TAKES = (4, 4, 4, 4)


def make_tiled(n):
    def swap(a, bit):
        return lax.ppermute(a, "rows", [(i, i ^ bit) for i in range(n)])

    def body(factor_panel, later_adjoint, saved_solution, cotangent, inverse_block):
        me = lax.axis_index("rows").astype(jnp.int32)
        own = cotangent.shape[0]
        ids = jnp.stack([me % 8, me // 8, me])

        half = own // 2
        again_inverse = lax.optimization_barrier(inverse_block)
        i2a = swap(upper(inverse_block), 2)
        i4 = swap(inverse_block, 4)
        i2b = swap(again_inverse[half:], 2)
        i6z = swap(i2a, 4)
        i6x = swap(i4[half:], 2)
        firsts = first(ids, later_adjoint, factor_panel, cotangent, (6, 4))
        firsts += again(ids, later_adjoint, factor_panel, cotangent, (2, 0))
        shards = []
        for q, at, a in ((0, 0, inverse_block), (4, 0, i4), (2, 0, i2a), (2, half, i2b), (6, 0, i6z), (6, half, i6x)):
            shards += [(q, at, a), (q + 1, at, swap(a, 1))]
        saved = order(ids, saved_solution)
        inv = gather(ids, shards)

        pieces = []
        acc = None
        for k in range(CHUNKS):
            kept = {}
            for j, g in enumerate((6, 4, 2, 0)):
                keep, send = firsts[(j * CHUNKS + k) * 2:(j * CHUNKS + k) * 2 + 2]
                kept[g] = keep + swap(send, 1).astype(F32)
            u4 = kept[4] + swap(kept[6].astype(BF), 2).astype(F32)
            u0 = kept[0] + swap(kept[2].astype(BF), 2).astype(F32)
            r = u0 + swap(u4.astype(BF), 4).astype(F32)
            r = (r + swap(r.astype(BF), 8).astype(F32)).astype(BF)
            pt = middle(ids, r, inv)
            p = {0: jnp.concatenate([pt, swap(pt, 8)], axis=1)}
            p[2] = swap(p[0], 2)
            p[4] = swap(p[0], 4)
            p[6] = swap(p[4], 2) if k < CHUNKS - 1 else swap(p[2], 4)
            for g in (0, 2, 4, 6):
                p[g + 1] = swap(p[g], 1)
            pieces.append([p[q] for q in range(8)])
        at = lo = 0
        for take in TAKES[:-1]:
            using = [pieces[c][q] for c, q in ORDER[at:at + take]]
            acc = outer(ids, saved, using, lo, acc)
            at += take
            lo += sum(p.shape[0] for p in using)
        grad, adj = last(ids, saved, acc, sum(pieces, []), TAKES[-1], lo, own)
        return adj, grad

    return body


def make_body(n):
    def swap(a, bit):
        return lax.ppermute(a, "rows", [(i, i ^ bit) for i in range(n)])

    rest = [8 << k for k in range(16) if 8 << k < n]

    def body(factor_panel, later_adjoint, saved_solution, cotangent, inverse_block):
        me = lax.axis_index("rows")
        low = me % 8
        sides, panel, own = later_adjoint.shape[1], factor_panel.shape[1], cotangent.shape[0]
        w = sides // 8

        def cols(a, q):
            return lax.dynamic_slice(a, (0, (low ^ q) * w), (a.shape[0], w))

        inv4 = swap(inverse_block, 4)
        kept = {}
        for g in (6, 2, 4, 0):
            pair = jnp.concatenate([cols(later_adjoint, g), cols(later_adjoint, g ^ 1)], axis=1)
            prod = dot(pair, factor_panel, 0, 0)
            cot = jnp.concatenate([cols(cotangent, g), cols(cotangent, g ^ 1)], axis=1).T
            base = lax.dynamic_update_slice(jnp.zeros((2 * w, panel), F32), cot, (0, me * own))
            both = base - prod
            got = swap(both[w:].astype(BF), 1)
            kept[g] = both[:w] + got.astype(F32)
        u4 = kept[4] + swap(kept[6].astype(BF), 2).astype(F32)
        u0 = kept[0] + swap(kept[2].astype(BF), 2).astype(F32)
        r = u0 + swap(u4.astype(BF), 4).astype(F32)
        shards = {0: inverse_block, 4: inv4, 2: swap(inverse_block, 2), 6: swap(inv4, 2)}
        inv = jnp.zeros((8 * own, panel), BF)
        for q in (0, 4, 2, 6):
            inv = lax.dynamic_update_slice(inv, shards[q], ((low ^ q) * own, 0))
            inv = lax.dynamic_update_slice(inv, swap(shards[q], 1), ((low ^ q ^ 1) * own, 0))
        for b in rest:
            r = r + swap(r.astype(BF), b).astype(F32)
        pt = dot(r.astype(BF), inv, 1, 1).astype(BF)
        for b in rest:
            other = swap(pt, b)
            up = (me // b) % 2
            pt = jnp.where(up == 1, jnp.concatenate([other, pt], 1), jnp.concatenate([pt, other], 1))
        p = {0: pt}
        p[2] = swap(pt, 2)
        p[4] = swap(pt, 4)
        p[6] = swap(p[4], 2)
        for g in (0, 4, 2, 6):
            p[g ^ 1] = swap(p[g], 1)
        left = jnp.concatenate([cols(saved_solution, q) for q in range(8)], axis=1)
        grad = -dot(left, jnp.concatenate([p[q] for q in range(8)], axis=0), 1, 0)
        adj = jnp.zeros((own, sides), BF)
        for q in range(8):
            mine = lax.dynamic_slice(p[q], (0, me * own), (w, own)).T
            adj = lax.dynamic_update_slice(adj, mine, (0, (low ^ q) * w))
        return adj, grad.astype(BF)

    return body


def solution(mesh):
    n = mesh.shape["rows"]
    placed = P(("groups", "rows"), None)
    return jax.shard_map(
        make_tiled(n) if n == 16 else make_body(n),
        mesh=mesh,
        in_specs=(placed,) * 5,
        out_specs=(placed, placed),
        check_vma=False,
    )
```
